32 devices in a mesh: groups: 2 (over y), expert: 8 (over z, x), section: 2 (over core).
Axes of the slice: x: 2, y: 2, z: 4, core: 2. Of those that a mesh axis runs over, the one named last changes fastest.
Arguments:
- tokens: bfloat16 [2, 128, 7168], P(None, ('groups', 'expert')), parts along dimension 1, may hold values from -6 to 6
- routes: int32 [2, 2, 128, 4], P('section', None, ('groups', 'expert')), parts along dimension 2, may hold values from 0 to 15, all different within a row; in each aligned block of 8 rows (0 to 7, 8 to 15, ..., all dimensions but the last counted through in order) at most 3 rows name the same one
- norm_gain: float32 [2, 7168], P('section'), may hold values from 0.5 to 1.5
- router_weight: bfloat16 [2, 7168, 16], P('section'), may hold values from -0.125 to 0.125
- gate_weight: bfloat16 [2, 7168, 16384], P('section', None, 'expert'), may hold values from -0.0625 to 0.0625
- up_weight: bfloat16 [2, 7168, 16384], P('section', None, 'expert'), may hold values from -0.0625 to 0.0625
- down_weight: bfloat16 [2, 16384, 7168], P('section', 'expert'), may hold values from -0.375 to 0.375
Outputs:
- encoded: bfloat16 [2, 128, 7168], P('section', ('groups', 'expert')), parts along dimension 1
The draws below stay inside these ranges and needn't reach their ends.
There are 2 independent parts, one for each index of `groups`. The reference program is written for one: setup_inputs(seed, part) draws one part's arguments, and reference() takes and returns one part's arrays. A program takes and returns all parts, laid end to end along the dimension named above; an argument that names none is the same for every part. Nothing has to cross between parts.
Inputs may be any that keep to these rules, and one draw needn't show every extreme that they name: `routes`: each token names 4 different experts. For every layer, micro-batch and aligned block of 8 tokens, no expert is named by more than 3 of the block's tokens.
All inputs are finite; a program needn't handle non-finite values.
Results may differ from the reference program's by a relative error of at most 0.0074.
Values may be sent and summed in bfloat16 or wider, within the bound.
A program may use at most 256 MiB of HBM per device.

```python
import math
import jax
import jax.numpy as jnp
import numpy as np
from jax import lax

D = 7168
FF = 1024
EXPERTS = 16
TOP = 4
TOK_DEV = 8
MB = 2
LAYERS = 2
TOKENS = 64
CAP = 3
N_EXPERT = 8


def level_of(own_key, extent, pieces, least, high):
    def one(dim, parts):
        steps = jax.random.uniform(jax.random.fold_in(jax.random.fold_in(own_key, 6), dim), (parts,), jnp.float32, least / len(pieces), high / len(pieces))
        return jnp.repeat(jnp.exp(steps), extent[dim] // parts).reshape((-1,) + (1,) * (len(extent) - dim - 1))

    gain = one(*pieces[0])
    for cut in pieces[1:]:
        gain = gain * one(*cut)
    return gain


def deal_out(stream_key, own, number, rows, amount, top, reach, lean):
    order = jax.random.permutation(stream_key, amount)
    packed, usual = shares(amount, rows * top, reach, lean, True), shares(amount, rows * top, reach, lean, False)
    places = jnp.arange(amount)

    def named(sizes, turn):
        used = int((sizes > 0).sum())
        fixed = max(1, used // 4)
        shifted = fixed + (places - fixed + turn * (used - fixed)) % max(1, amount - fixed)
        return jnp.zeros((amount,), jnp.int32).at[order[jnp.where(places < fixed, places, shifted)]].set(jnp.asarray(sizes, jnp.int32))

    sizes = jnp.where(number % 4 == 0, named(packed, number // 4), named(usual, number - number // 4 - 1))
    mixed = jax.random.permutation(jax.random.fold_in(own, 3), amount)
    source_of, taker = mixed[0:amount // 2 * 2:2], mixed[1:amount // 2 * 2:2]
    slack = jnp.minimum(sizes[source_of] - 1, reach - sizes[taker]) // 2
    slack = jnp.where((source_of == order[0]) | (taker == order[0]) | (sizes[taker] == 0), 0, jnp.maximum(slack, 0))
    shifted = jax.random.randint(jax.random.fold_in(own, 4), (amount // 2,), 0, 1 << 20) % (slack + 1)
    sizes = sizes.at[source_of].add(-shifted).at[taker].add(shifted)
    labels = jnp.searchsorted(jnp.cumsum(sizes), jnp.arange(rows * top), side="right").astype(jnp.int32)
    grid = labels.reshape(top, rows).T
    grid = grid[jax.random.permutation(jax.random.fold_in(own, 1), rows)]
    turn = jax.random.randint(jax.random.fold_in(own, 2), (rows, 1), 0, top)
    return jnp.take_along_axis(grid, (jnp.arange(top)[None, :] + turn) % top, axis=1)


def shares(amount, total, reach, slope, full):
    weights = [(1 << 20) // math.isqrt(rank ** slope) + 1 for rank in range(1, amount + 1)]
    largest = reach if full else min(reach, max(-(-total // amount), total * weights[0] // sum(weights)))
    least = 1 if total - largest >= amount - 1 else 0
    counts, surplus = [largest] + [least] * (amount - 1), total - largest - least * (amount - 1)
    while surplus > 0:
        candidates = [i for i in range(1, amount) if counts[i] < largest] or [i for i in range(1, amount) if counts[i] < reach]
        whole, left = sum([weights[i] for i in candidates]), surplus
        for i in candidates:
            extra = min(reach - counts[i], max(1, left * weights[i] // whole), surplus)
            counts[i] = counts[i] + extra
            surplus = surplus - extra
    return np.array(counts)


def normal_values(key, shape, spread, most, split=(), kind=jnp.bfloat16):
    array = jax.random.normal(key, shape, jnp.float32) * spread
    if len(split) > 0:
        array = level_of(key, shape, split, -0.22, 0.18) * array
    return jnp.clip(array, min=-most, max=most).astype(kind)


def setup_inputs(seed: int = 0, part: int = 0) -> dict:
    streams_of = jax.random.split(jax.random.key(seed), 8)
    part_keys = jax.random.split(jax.random.fold_in(streams_of[7], part), 8)
    tokens = normal_values(part_keys[0], (MB, TOKENS, D), 1.0, 6.0, ((1, 8),))
    routes_keys = jax.random.split(jax.random.fold_in(part_keys[1], 1), LAYERS * MB * TOKENS // TOK_DEV)
    routes_turns = jax.random.permutation(jax.random.fold_in(part_keys[1], 3), LAYERS * MB * TOKENS // TOK_DEV)
    routes = jax.vmap(lambda own, number: deal_out(jax.random.fold_in(part_keys[1], 2), own, number, TOK_DEV, EXPERTS, TOP, CAP, 2))(routes_keys, routes_turns).reshape((LAYERS, MB, TOKENS, TOP))
    norm_gain = jnp.clip(0.5 + 1.0 * jax.random.uniform(streams_of[2], (LAYERS, D), jnp.float32) ** level_of(streams_of[2], (LAYERS, D), ((0, 2),), -0.2, 0.2), 0.5, 1.5)
    router_weight = normal_values(streams_of[3], (LAYERS, D, EXPERTS), (D // 4) ** -0.5, 0.125, ((0, 2),))
    gate_weight = normal_values(streams_of[4], (LAYERS, D, EXPERTS * FF), D ** -0.5, 0.0625, ((0, 2), (2, 8)))
    up_weight = normal_values(streams_of[5], (LAYERS, D, EXPERTS * FF), D ** -0.5, 0.0625, ((0, 2), (2, 8)))
    down_weight = normal_values(streams_of[6], (LAYERS, EXPERTS * FF, D), (FF // 4) ** -0.5, 0.375, ((0, 2), (1, 8)))
    return {"tokens": tokens, "routes": routes, "norm_gain": norm_gain, "router_weight": router_weight, "gate_weight": gate_weight, "up_weight": up_weight, "down_weight": down_weight}


EPSILON = 1e-06

def moe_layer(token_rows, routes, gain_row, router_weight, gate_weight, up_weight, down_weight):
    micro_count, row_count, model_width = token_rows.shape
    total_rows = micro_count * row_count
    values = token_rows.astype(jnp.float32).reshape(total_rows, model_width)
    factor = lax.rsqrt(lax.optimization_barrier(jnp.mean(values * values, axis=-1, keepdims=True)) + EPSILON)
    normed = (values * factor * gain_row).astype(jnp.bfloat16)
    logits = jnp.dot(normed, router_weight, preferred_element_type=jnp.float32)
    affinity = jax.nn.sigmoid(logits)
    flat_routes = routes.reshape(total_rows, TOP)
    expert_hit = (flat_routes[..., None] == jnp.arange(EXPERTS, dtype=jnp.int32)).astype(jnp.float32)
    picked = lax.optimization_barrier(jnp.sum(expert_hit * affinity[:, None, :], axis=-1))
    gate_vals = picked / lax.optimization_barrier(jnp.sum(picked, axis=-1, keepdims=True))
    expert_gate = lax.optimization_barrier(jnp.sum(expert_hit * gate_vals[..., None], axis=1))
    routed = lax.optimization_barrier(jnp.sum(expert_hit, axis=1))
    row_limit = MB * N_EXPERT * CAP
    shards = max(1, N_EXPERT // EXPERTS)
    unit_width = FF // shards

    def one_expert(expert_idx):
        gate_block = lax.dynamic_slice_in_dim(gate_weight, expert_idx * FF, FF, 1).astype(jnp.float32)
        up_block = lax.dynamic_slice_in_dim(up_weight, expert_idx * FF, FF, 1).astype(jnp.float32)
        down_block = lax.dynamic_slice_in_dim(down_weight, expert_idx * FF, FF, 0).astype(jnp.float32)
        member = routed[:, expert_idx]
        row_index = jnp.nonzero(member > 0, size=row_limit, fill_value=0)[0].astype(jnp.int32)
        live_rows = (jnp.arange(row_limit) < jnp.sum(member)).astype(jnp.float32)
        chosen = normed[row_index].astype(jnp.float32)
        gate_part = jnp.dot(chosen, gate_block)
        up_part = jnp.dot(chosen, up_block)
        hidden = (jax.nn.silu(gate_part) * up_part).astype(jnp.bfloat16)
        hidden = lax.optimization_barrier(hidden).astype(jnp.float32).reshape(row_limit, shards, unit_width)
        partial_value = jnp.einsum('rsf,sfd->rsd', hidden, down_block.reshape(shards, unit_width, model_width))
        partial_value = lax.optimization_barrier(partial_value.astype(jnp.bfloat16)).astype(jnp.float32)
        scale = expert_gate[:, expert_idx][row_index] * live_rows
        weighted_sum = lax.optimization_barrier(jnp.sum(partial_value, axis=1)) * scale[:, None]
        return (row_index, weighted_sum)
    indices, totals = lax.map(one_expert, jnp.arange(EXPERTS, dtype=jnp.int32))
    branch = jnp.zeros((total_rows, model_width), jnp.float32).at[indices.reshape(-1)].add(totals.reshape(-1, model_width))
    return (values + branch).astype(jnp.bfloat16).reshape(micro_count, row_count, model_width)

def reference(tokens, routes, norm_gain, router_weight, gate_weight, up_weight, down_weight):
    hidden_state = tokens
    for layer_idx in range(LAYERS):
        hidden_state = moe_layer(hidden_state, routes[layer_idx], norm_gain[layer_idx], router_weight[layer_idx], gate_weight[layer_idx], up_weight[layer_idx], down_weight[layer_idx])
    return hidden_state
```

```python
import functools

import jax
import jax.numpy as jnp
from jax import lax
from jax.experimental import pallas as pl
from jax.experimental.pallas import tpu as pltpu
from jax.sharding import PartitionSpec as P

EPSILON = 1e-06
MESH = pl.DeviceIdType.MESH
LANES = 128


def largest_divisor(value, most):
    return next(d for d in range(min(value, most), 0, -1) if value % d == 0)


def kernel(
    count, unit_width, slots_gu, slots_d,
    tokens, hit, gain, router, gate_hbm, up_hbm, down_hbm, out,
    x, g, gates, hidden, wgu, wd, y, rx, rz, res, fin,
    sem_gu, sem_d, gather_send, gather_recv, fwd_send, fwd_recv,
    pair_send, pair_recv, line_send, line_recv, pass_send, pass_recv,
):
    me = lax.axis_index("expert")
    sec = lax.axis_index("section")
    line = count // 2
    col, pos = lax.rem(me, 2), lax.div(me, 2)
    other = 1 - col
    width = x.shape[-1]
    tile_f = wgu.shape[-1]
    tile_d = wd.shape[-1]
    ff_local = hidden.shape[-1]
    steps_f = ff_local // tile_f
    steps_d = width // tile_d
    rows = g.shape[2]
    total = count * rows
    half = rows // 2
    partner = {"expert": pos * 2 + other}
    across = {"section": 1 - sec}

    def member(p):
        return {"expert": p * 2 + col}

    def load_gu(f, which, start):
        slot = lax.rem(f, slots_gu)
        source = (gate_hbm, up_hbm)[which]
        copy = pltpu.make_async_copy(
            source.at[0, :, pl.ds(pl.multiple_of(f * tile_f, tile_f), tile_f)],
            wgu.at[slot, which],
            sem_gu.at[slot, which],
        )
        copy.start() if start else copy.wait()

    def load_d(c, start):
        slot = lax.rem(c, slots_d)
        copy = pltpu.make_async_copy(
            down_hbm.at[0, :, pl.ds(pl.multiple_of(c * tile_d, tile_d), tile_d)],
            wd.at[slot],
            sem_d.at[slot],
        )
        copy.start() if start else copy.wait()

    for f in range(slots_gu):
        load_gu(f, 0, True)
        load_gu(f, 1, True)
    for c in range(slots_d):
        load_d(c, True)

    barrier = pltpu.get_barrier_semaphore()
    for k in range(1, line):
        pl.semaphore_signal(barrier, inc=1, device_id=member(lax.rem(pos + k, line)), device_id_type=MESH)
    pl.semaphore_signal(barrier, inc=1, device_id=partner, device_id_type=MESH)
    pl.semaphore_signal(barrier, inc=1, device_id=across, device_id_type=MESH)
    pl.semaphore_wait(barrier, line + 1)

    def remote(src, dst, send, recv, device):
        return pltpu.make_async_remote_copy(
            src_ref=src, dst_ref=dst, send_sem=send, recv_sem=recv,
            device_id=device, device_id_type=MESH,
        )

    def pass_on():
        return remote(res, x, pass_send.at[0], pass_recv.at[0], across)

    def give_back():
        return remote(res.at[0], fin, pass_send.at[1], pass_recv.at[1], across)

    @pl.when(sec == 0)
    def _():
        x[...] = tokens[...]

    @pl.when(sec == 1)
    def _():
        pass_on().wait_recv()

    for m in range(2):
        values = x[m].astype(jnp.float32)
        factor = lax.rsqrt(jnp.mean(values * values, axis=-1, keepdims=True) + EPSILON)
        g[col, pos, m * half:(m + 1) * half, 0:width] = (values * factor * gain[...]).astype(jnp.bfloat16)
    g[col, pos, :, width:width + LANES] = hit[...]

    def to_member(k):
        block = g.at[col, pos]
        return remote(block, block, gather_send.at[k], gather_recv.at[k], member(lax.rem(pos + k, line)))

    def from_member(k):
        block = g.at[col, lax.rem(pos + line - k, line)]
        return remote(block, block, gather_send.at[k], gather_recv.at[k], partner)

    def to_partner(k):
        block = g.at[col, lax.rem(pos + line - k, line)]
        return remote(block, block, fwd_send.at[k], fwd_recv.at[k], partner)

    def from_partner(k):
        block = g.at[other, lax.rem(pos + line - k, line)]
        return remote(block, block, fwd_send.at[k], fwd_recv.at[k], partner)

    to_partner(0).start()
    for k in range(1, line):
        to_member(k).start()
    for k in range(1, line):
        from_member(k).wait_recv()
        to_partner(k).start()
    for k in range(line):
        from_partner(k).wait_recv()

    def all_rows():
        return g[:, :, :, 0:width].reshape(total, width)

    experts = router.shape[-1]
    logits = jnp.dot(all_rows(), router[0], preferred_element_type=jnp.float32)
    routed = g[:, :, :, width:width + LANES].reshape(total, LANES)[:, 0:experts].astype(jnp.float32)
    picked = jax.nn.sigmoid(logits) * routed
    gates[...] = picked / jnp.sum(picked, axis=-1, keepdims=True)

    def up_step(f, carry):
        slot = lax.rem(f, slots_gu)
        load_gu(f, 0, False)
        load_gu(f, 1, False)
        lhs = all_rows()
        gate_part = jnp.dot(lhs, wgu[slot, 0], preferred_element_type=jnp.float32)
        up_part = jnp.dot(lhs, wgu[slot, 1], preferred_element_type=jnp.float32)
        expert = lax.div(me * ff_local + f * tile_f, unit_width)
        lane = lax.broadcasted_iota(jnp.int32, (total, experts), 1)
        scale = jnp.sum(jnp.where(lane == expert, gates[...], 0.0), axis=-1, keepdims=True)
        value = gate_part / (1.0 + jnp.exp(-gate_part)) * up_part * scale
        hidden[:, pl.ds(pl.multiple_of(f * tile_f, tile_f), tile_f)] = value.astype(jnp.bfloat16)

        @pl.when(f + slots_gu < steps_f)
        def _():
            load_gu(f + slots_gu, 0, True)
            load_gu(f + slots_gu, 1, True)

        return carry

    lax.fori_loop(0, steps_f, up_step, 0)

    def pair_copy(c):
        return remote(y.at[c, other], rx.at[c], pair_send.at[c], pair_recv.at[c], partner)

    def line_copy(c, k):
        p = lax.rem(pos + k, line)
        return remote(y.at[c, col, p], rz.at[c, k - 1], line_send.at[c, k - 1], line_recv.at[c, k - 1], member(p))

    def line_step(c):
        pair_copy(c).wait_recv()
        y[c, col] = (y[c, col].astype(jnp.float32) + rx[c].astype(jnp.float32)).astype(jnp.bfloat16)
        for k in range(1, line):
            line_copy(c, k).start()

    def down_step(c, carry):
        load_d(c, False)
        part = jnp.dot(hidden[...], wd[lax.rem(c, slots_d)], preferred_element_type=jnp.float32)
        y[c] = part.astype(jnp.bfloat16).reshape(2, line, rows, tile_d)
        pair_copy(c).start()

        @pl.when(c + slots_d < steps_d)
        def _():
            load_d(c + slots_d, True)

        @pl.when(c >= 1)
        def _():
            line_step(c - 1)

        return carry

    lax.fori_loop(0, steps_d, down_step, 0)
    line_step(steps_d - 1)

    def finish_step(c, carry):
        at = pl.ds(pl.multiple_of(c * tile_d, tile_d), tile_d)
        branch = y[c, col, pos].astype(jnp.float32)
        for k in range(1, line):
            line_copy(c, k).wait_recv()
            branch = branch + rz[c, k - 1].astype(jnp.float32)
        for m in range(2):
            res[m, :, at] = (x[m, :, at].astype(jnp.float32) + branch[m * half:(m + 1) * half]).astype(jnp.bfloat16)
        return carry

    lax.fori_loop(0, steps_d, finish_step, 0)

    @pl.when(sec == 0)
    def _():
        pass_on().start()

    @pl.when(sec == 1)
    def _():
        give_back().start()

    for k in range(1, line):
        to_member(k).wait_send()
    for k in range(line):
        to_partner(k).wait_send()

    def drain_step(c, carry):
        pair_copy(c).wait_send()
        for k in range(1, line):
            line_copy(c, k).wait_send()
        return carry

    lax.fori_loop(0, steps_d, drain_step, 0)

    @pl.when(sec == 0)
    def _():
        pass_on().wait_send()
        give_back().wait_recv()
        out[0] = fin[...]

    @pl.when(sec == 1)
    def _():
        out[0] = res[1]
        give_back().wait_send()


def local(count, tokens, routes, norm_gain, router_weight, gate_weight, up_weight, down_weight):
    micro, per_block, width = tokens.shape
    rows = micro * per_block
    experts = router_weight.shape[-1]
    ff_local = gate_weight.shape[-1]
    unit_width = ff_local * count // experts
    line = count // 2
    tile_f = largest_divisor(min(unit_width, ff_local), 256)
    tile_d = largest_divisor(width, 512)
    steps_f, steps_d = ff_local // tile_f, width // tile_d
    slots_gu, slots_d = min(steps_f, 5), min(steps_d, 6)
    picks = routes[0].reshape(rows, routes.shape[-1])
    hit = jnp.sum(
        (picks[:, :, None] == jnp.arange(LANES, dtype=jnp.int32)).astype(jnp.float32), axis=1
    ).astype(jnp.bfloat16)
    dma = pltpu.SemaphoreType.DMA
    vmem = pl.BlockSpec(memory_space=pltpu.VMEM)
    anyspace = pl.BlockSpec(memory_space=pl.ANY)
    bf16 = jnp.bfloat16
    return pl.pallas_call(
        functools.partial(kernel, count, unit_width, slots_gu, slots_d),
        out_shape=jax.ShapeDtypeStruct((1, per_block, width), bf16),
        in_specs=[vmem, vmem, vmem, vmem, anyspace, anyspace, anyspace],
        out_specs=vmem,
        scratch_shapes=[
            pltpu.VMEM((micro, per_block, width), bf16),
            pltpu.VMEM((2, line, rows, width + LANES), bf16),
            pltpu.VMEM((count * rows, experts), jnp.float32),
            pltpu.VMEM((count * rows, ff_local), bf16),
            pltpu.VMEM((slots_gu, 2, width, tile_f), bf16),
            pltpu.VMEM((slots_d, ff_local, tile_d), bf16),
            pltpu.VMEM((steps_d, 2, line, rows, tile_d), bf16),
            pltpu.VMEM((steps_d, line, rows, tile_d), bf16),
            pltpu.VMEM((steps_d, line - 1, rows, tile_d), bf16),
            pltpu.VMEM((micro, per_block, width), bf16),
            pltpu.VMEM((per_block, width), bf16),
            dma((slots_gu, 2)),
            dma((slots_d,)),
            dma((line,)),
            dma((line,)),
            dma((line,)),
            dma((line,)),
            dma((steps_d,)),
            dma((steps_d,)),
            dma((steps_d, line - 1)),
            dma((steps_d, line - 1)),
            dma((2,)),
            dma((2,)),
        ],
        compiler_params=pltpu.CompilerParams(
            collective_id=0, has_side_effects=True, vmem_limit_bytes=67043328
        ),
    )(tokens, hit, norm_gain, router_weight, gate_weight, up_weight, down_weight)


def solution(mesh):
    placed = (
        P(None, ("groups", "expert"), None),
        P("section", None, ("groups", "expert"), None),
        P("section", None),
        P("section", None, None),
        P("section", None, "expert"),
        P("section", None, "expert"),
        P("section", "expert", None),
    )
    return jax.shard_map(
        functools.partial(local, mesh.shape["expert"]),
        mesh=mesh,
        in_specs=placed,
        out_specs=P("section", ("groups", "expert"), None),
        check_vma=False,
    )
```

```python
import functools

import jax
import jax.numpy as jnp
from jax import lax
from jax.experimental import pallas as pl
from jax.experimental.pallas import tpu as pltpu
from jax.sharding import PartitionSpec as P

EPSILON = 1e-06
MESH = pl.DeviceIdType.MESH
LANES = 128
LAG = 5
AHEAD = 2


def largest_divisor(value, most):
    return next(d for d in range(min(value, most), 0, -1) if value % d == 0)


def kernel(
    count, unit_width, slots_gu, slots_d,
    tokens, hit, gain, router, gate_hbm, up_hbm, down_hbm, out,
    x, g, marks, logits, acc, hidden, wgu, wd, y, rx, rz, res, fin,
    sem_gu, sem_d, gather_send, gather_recv, fwd_send, fwd_recv,
    pair_send, pair_recv, line_send, line_recv, pass_send, pass_recv,
):
    me = lax.axis_index("expert")
    sec = lax.axis_index("section")
    line = count // 2
    col, pos = lax.rem(me, 2), lax.div(me, 2)
    other = 1 - col
    width = x.shape[-1]
    tile_k = wgu.shape[1]
    tile_f = largest_divisor(min(unit_width, wgu.shape[-1]), 512)
    steps_k = width // tile_k
    tile_d = wd.shape[-1]
    ff_local = hidden.shape[-1]
    steps_f = ff_local // tile_f
    loads = 2 * steps_k
    steps_d = width // tile_d
    rows = g.shape[3]
    total = count * rows
    half = rows // 2
    partner = {"expert": pos * 2 + other}
    across = {"section": 1 - sec}

    def member(p):
        return {"expert": p * 2 + col}

    def load_gu(k, which, start):
        slot = lax.rem(2 * k + which, slots_gu)
        source = (gate_hbm, up_hbm)[which]
        copy = pltpu.make_async_copy(
            source.at[0, pl.ds(pl.multiple_of(k * tile_k, tile_k), tile_k), :],
            wgu.at[slot],
            sem_gu.at[slot],
        )
        copy.start() if start else copy.wait()

    def load_d(c, start):
        slot = lax.rem(c, slots_d)
        copy = pltpu.make_async_copy(
            down_hbm.at[0, :, pl.ds(pl.multiple_of(c * tile_d, tile_d), tile_d)],
            wd.at[slot],
            sem_d.at[slot],
        )
        copy.start() if start else copy.wait()

    for number in range(slots_gu):
        load_gu(number // 2, number % 2, True)

    def first_down():
        for c in range(slots_d):
            load_d(c, True)

    @pl.when(sec == 1)
    def _():
        first_down()

    barrier = pltpu.get_barrier_semaphore()
    for k in range(1, line):
        pl.semaphore_signal(barrier, inc=1, device_id=member(lax.rem(pos + k, line)), device_id_type=MESH)
    pl.semaphore_signal(barrier, inc=1, device_id=partner, device_id_type=MESH)
    pl.semaphore_signal(barrier, inc=1, device_id=across, device_id_type=MESH)
    pl.semaphore_wait(barrier, line + 1)

    def remote(src, dst, send, recv, device):
        return pltpu.make_async_remote_copy(
            src_ref=src, dst_ref=dst, send_sem=send, recv_sem=recv,
            device_id=device, device_id_type=MESH,
        )

    def pass_on():
        return remote(res, x, pass_send.at[0], pass_recv.at[0], across)

    def give_back():
        return remote(res.at[0], fin, pass_send.at[1], pass_recv.at[1], across)

    def block_of(k, c, p):
        return g.at[k, c, p] if k is not None else marks.at[c, p]

    def sem_of(k):
        return k if k is not None else steps_k

    def to_member(k, j):
        block = block_of(k, col, pos)
        return remote(block, block, gather_send.at[sem_of(k), j], gather_recv.at[sem_of(k), j], member(lax.rem(pos + j, line)))

    def from_member(k, j):
        block = block_of(k, col, lax.rem(pos + line - j, line))
        return remote(block, block, gather_send.at[sem_of(k), j], gather_recv.at[sem_of(k), j], partner)

    def to_partner(k, j):
        block = block_of(k, col, lax.rem(pos + line - j, line))
        return remote(block, block, fwd_send.at[sem_of(k), j], fwd_recv.at[sem_of(k), j], partner)

    def from_partner(k, j):
        block = block_of(k, other, lax.rem(pos + line - j, line))
        return remote(block, block, fwd_send.at[sem_of(k), j], fwd_recv.at[sem_of(k), j], partner)

    def send_own(k):
        for j in range(1, line):
            to_member(k, j).start()
        to_partner(k, 0).start()

    def forward(k):
        for j in range(1, line):
            from_member(k, j).wait_recv()
            to_partner(k, j).start()

    def receive(k):
        for j in range(line):
            from_partner(k, j).wait_recv()

    marks[col, pos] = hit[...]
    send_own(None)

    @pl.when(sec == 0)
    def _():
        x[...] = tokens[...]

    @pl.when(sec == 1)
    def _():
        pass_on().wait_recv()

    factors = []
    for m in range(2):
        values = x[m].astype(jnp.float32)
        factors.append(lax.rsqrt(jnp.mean(values * values, axis=-1, keepdims=True) + EPSILON))
    for k in range(steps_k):
        for m in range(2):
            values = x[m, :, k * tile_k:(k + 1) * tile_k].astype(jnp.float32)
            normed = values * factors[m] * gain[:, k * tile_k:(k + 1) * tile_k]
            g[k, col, pos, m * half:(m + 1) * half, :] = normed.astype(jnp.bfloat16)
        send_own(k)

    experts = router.shape[1]
    acc[...] = jnp.zeros_like(acc)
    logits[...] = jnp.zeros_like(logits)
    forward(None)
    ahead = min(steps_k, AHEAD)
    for k in range(ahead):
        forward(k)

    def up_step(k, carry):
        @pl.when(k + ahead < steps_k)
        def _():
            forward(k + ahead)

        receive(k)
        lhs = g[k].reshape(total, tile_k)
        at = pl.ds(pl.multiple_of(k * tile_k, tile_k), tile_k)
        logits[...] += lax.dot_general(
            lhs, router[0, :, at], (((1,), (1,)), ((), ())), preferred_element_type=jnp.float32
        )
        for which in range(2):
            load_gu(k, which, False)
            slot = lax.rem(2 * k + which, slots_gu)
            for f in range(steps_f):
                cut = slice(f * tile_f, (f + 1) * tile_f)
                acc[which, :, cut] += jnp.dot(lhs, wgu[slot, :, cut], preferred_element_type=jnp.float32)
            later = 2 * k + which + slots_gu

            @pl.when(later < loads)
            def _():
                if slots_gu % 2 == 0:
                    load_gu(k + slots_gu // 2, which, True)
                elif which == 0:
                    load_gu(k + slots_gu // 2, 1, True)
                else:
                    load_gu(k + slots_gu // 2 + 1, 0, True)

        @pl.when((sec == 0) & (k == start_down))
        def _():
            first_down()

        return carry

    start_down = max(0, (loads - slots_gu - 1) // 2)
    lax.fori_loop(0, steps_k, up_step, 0)

    receive(None)
    routed = marks[...].reshape(total, LANES)[:, 0:experts].astype(jnp.float32)
    picked = jax.nn.sigmoid(logits[...]) * routed
    gates = picked / jnp.sum(picked, axis=-1, keepdims=True)
    lane = lax.broadcasted_iota(jnp.int32, (total, experts), 1)
    for f in range(steps_f):
        cut = slice(f * tile_f, (f + 1) * tile_f)
        expert = lax.div(me * ff_local + f * tile_f, unit_width)
        scale = jnp.sum(jnp.where(lane == expert, gates, 0.0), axis=-1, keepdims=True)
        gate_part = acc[0, :, cut]
        value = gate_part / (1.0 + jnp.exp(-gate_part)) * acc[1, :, cut] * scale
        hidden[:, cut] = value.astype(jnp.bfloat16)

    def pair_copy(c):
        return remote(y.at[c, other], rx.at[c], pair_send.at[c], pair_recv.at[c], partner)

    def line_copy(c, k):
        p = lax.rem(pos + k, line)
        return remote(y.at[c, col, p], rz.at[c, k - 1], line_send.at[c, k - 1], line_recv.at[c, k - 1], member(p))

    def line_step(c):
        pair_copy(c).wait_recv()
        y[c, col] = (y[c, col].astype(jnp.float32) + rx[c].astype(jnp.float32)).astype(jnp.bfloat16)
        for k in range(1, line):
            line_copy(c, k).start()

    def down_step(c, carry):
        load_d(c, False)
        part = jnp.dot(hidden[...], wd[lax.rem(c, slots_d)], preferred_element_type=jnp.float32)
        y[c] = part.astype(jnp.bfloat16).reshape(2, line, rows, tile_d)
        pair_copy(c).start()

        @pl.when(c + slots_d < steps_d)
        def _():
            load_d(c + slots_d, True)

        @pl.when(c >= lag_d)
        def _():
            line_step(c - lag_d)

        return carry

    def late_step(c, carry):
        line_step(c)
        return carry

    lag_d = min(steps_d, LAG)
    lax.fori_loop(0, steps_d, down_step, 0)
    lax.fori_loop(steps_d - lag_d, steps_d, late_step, 0)

    def finish_step(c, carry):
        at = pl.ds(pl.multiple_of(c * tile_d, tile_d), tile_d)
        branch = y[c, col, pos].astype(jnp.float32)
        for k in range(1, line):
            line_copy(c, k).wait_recv()
            branch = branch + rz[c, k - 1].astype(jnp.float32)
        for m in range(2):
            res[m, :, at] = (x[m, :, at].astype(jnp.float32) + branch[m * half:(m + 1) * half]).astype(jnp.bfloat16)
        return carry

    lax.fori_loop(0, steps_d, finish_step, 0)

    @pl.when(sec == 0)
    def _():
        pass_on().start()

    @pl.when(sec == 1)
    def _():
        give_back().start()

    def drain_own(k):
        for j in range(1, line):
            to_member(k, j).wait_send()
        for j in range(line):
            to_partner(k, j).wait_send()

    def drain_chunk(k, carry):
        drain_own(k)
        return carry

    drain_own(None)
    lax.fori_loop(0, steps_k, drain_chunk, 0)

    def drain_step(c, carry):
        pair_copy(c).wait_send()
        for k in range(1, line):
            line_copy(c, k).wait_send()
        return carry

    lax.fori_loop(0, steps_d, drain_step, 0)

    @pl.when(sec == 0)
    def _():
        pass_on().wait_send()
        give_back().wait_recv()
        out[0] = fin[...]

    @pl.when(sec == 1)
    def _():
        out[0] = res[1]
        give_back().wait_send()


def local(count, tokens, routes, norm_gain, router_weight, gate_weight, up_weight, down_weight):
    micro, per_block, width = tokens.shape
    rows = micro * per_block
    experts = router_weight.shape[-1]
    ff_local = gate_weight.shape[-1]
    unit_width = ff_local * count // experts
    line = count // 2
    tile_k = largest_divisor(width, 1024)
    tile_d = largest_divisor(width, 512)
    steps_k, steps_d = width // tile_k, width // tile_d
    slots_gu, slots_d = min(2 * steps_k, 9), min(steps_d, 6)
    picks = routes[0].reshape(rows, routes.shape[-1])
    hit = jnp.sum(
        (picks[:, :, None] == jnp.arange(LANES, dtype=jnp.int32)).astype(jnp.float32), axis=1
    ).astype(jnp.bfloat16)
    dma = pltpu.SemaphoreType.DMA
    vmem = pl.BlockSpec(memory_space=pltpu.VMEM)
    anyspace = pl.BlockSpec(memory_space=pl.ANY)
    bf16 = jnp.bfloat16
    return pl.pallas_call(
        functools.partial(kernel, count, unit_width, slots_gu, slots_d),
        out_shape=jax.ShapeDtypeStruct((1, per_block, width), bf16),
        in_specs=[vmem, vmem, vmem, vmem, anyspace, anyspace, anyspace],
        out_specs=vmem,
        scratch_shapes=[
            pltpu.VMEM((micro, per_block, width), bf16),
            pltpu.VMEM((steps_k, 2, line, rows, tile_k), bf16),
            pltpu.VMEM((2, line, rows, LANES), bf16),
            pltpu.VMEM((count * rows, experts), jnp.float32),
            pltpu.VMEM((2, count * rows, ff_local), jnp.float32),
            pltpu.VMEM((count * rows, ff_local), bf16),
            pltpu.VMEM((slots_gu, tile_k, ff_local), bf16),
            pltpu.VMEM((slots_d, ff_local, tile_d), bf16),
            pltpu.VMEM((steps_d, 2, line, rows, tile_d), bf16),
            pltpu.VMEM((steps_d, line, rows, tile_d), bf16),
            pltpu.VMEM((steps_d, line - 1, rows, tile_d), bf16),
            pltpu.VMEM((micro, per_block, width), bf16),
            pltpu.VMEM((per_block, width), bf16),
            dma((slots_gu,)),
            dma((slots_d,)),
            dma((steps_k + 1, line)),
            dma((steps_k + 1, line)),
            dma((steps_k + 1, line)),
            dma((steps_k + 1, line)),
            dma((steps_d,)),
            dma((steps_d,)),
            dma((steps_d, line - 1)),
            dma((steps_d, line - 1)),
            dma((2,)),
            dma((2,)),
        ],
        compiler_params=pltpu.CompilerParams(
            collective_id=0, has_side_effects=True, vmem_limit_bytes=67043328
        ),
    )(tokens, hit, norm_gain, jnp.swapaxes(router_weight, 1, 2), gate_weight, up_weight, down_weight)


def solution(mesh):
    placed = (
        P(None, ("groups", "expert"), None),
        P("section", None, ("groups", "expert"), None),
        P("section", None),
        P("section", None, None),
        P("section", None, "expert"),
        P("section", None, "expert"),
        P("section", "expert", None),
    )
    return jax.shard_map(
        functools.partial(local, mesh.shape["expert"]),
        mesh=mesh,
        in_specs=placed,
        out_specs=P("section", ("groups", "expert"), None),
        check_vma=False,
    )
```

```python
import functools

import jax
import jax.numpy as jnp
from jax import lax
from jax.experimental import pallas as pl
from jax.experimental.pallas import tpu as pltpu
from jax.sharding import PartitionSpec as P

EPSILON = 1e-06
MESH = pl.DeviceIdType.MESH
LANES = 128
LAG = 5
AHEAD = 2


def largest_divisor(value, most):
    return next(d for d in range(min(value, most), 0, -1) if value % d == 0)


def kernel(
    count, unit_width, slots_gu, slots_d,
    tokens, hit, gain, router, gate_hbm, up_hbm, down_hbm, out,
    x, g, marks, logits, acc, hidden, wgu, wd, y, rx, rz, res, fin,
    sem_gu, sem_d, gather_send, gather_recv, fwd_send, fwd_recv,
    pair_send, pair_recv, line_send, line_recv, pass_send, pass_recv,
):
    me = lax.axis_index("expert")
    sec = lax.axis_index("section")
    line = count // 2
    col, pos = lax.rem(me, 2), lax.div(me, 2)
    other = 1 - col
    width = x.shape[-1]
    tile_k = wgu.shape[1]
    tile_f = largest_divisor(min(unit_width, wgu.shape[-1]), 512)
    steps_k = width // tile_k
    tile_d = wd.shape[-1]
    ff_local = hidden.shape[-1]
    steps_f = ff_local // tile_f
    loads = 2 * steps_k
    steps_d = width // tile_d
    rows = g.shape[3]
    total = count * rows
    half = rows // 2
    partner = {"expert": pos * 2 + other}
    across = {"section": 1 - sec}

    def member(p):
        return {"expert": p * 2 + col}

    def load_gu(k, which, start):
        slot = lax.rem(2 * k + which, slots_gu)
        source = (gate_hbm, up_hbm)[which]
        copy = pltpu.make_async_copy(
            source.at[0, pl.ds(pl.multiple_of(k * tile_k, tile_k), tile_k), :],
            wgu.at[slot],
            sem_gu.at[slot],
        )
        copy.start() if start else copy.wait()

    def load_d(c, start):
        slot = lax.rem(c, slots_d)
        copy = pltpu.make_async_copy(
            down_hbm.at[0, :, pl.ds(pl.multiple_of(c * tile_d, tile_d), tile_d)],
            wd.at[slot],
            sem_d.at[slot],
        )
        copy.start() if start else copy.wait()

    for number in range(slots_gu):
        load_gu(number // 2, number % 2, True)

    def first_down():
        for c in range(slots_d):
            load_d(c, True)

    @pl.when(sec == 1)
    def _():
        first_down()

    barrier = pltpu.get_barrier_semaphore()
    for k in range(1, line):
        pl.semaphore_signal(barrier, inc=1, device_id=member(lax.rem(pos + k, line)), device_id_type=MESH)
    pl.semaphore_signal(barrier, inc=1, device_id=partner, device_id_type=MESH)
    pl.semaphore_signal(barrier, inc=1, device_id=across, device_id_type=MESH)
    pl.semaphore_wait(barrier, line + 1)

    def remote(src, dst, send, recv, device):
        return pltpu.make_async_remote_copy(
            src_ref=src, dst_ref=dst, send_sem=send, recv_sem=recv,
            device_id=device, device_id_type=MESH,
        )

    def columns(c):
        return pl.ds(pl.multiple_of(c * tile_d, tile_d), tile_d)

    def pass_on(c):
        cut = columns(c)
        return remote(res.at[:, :, cut], x.at[:, :, cut], pass_send.at[0, c], pass_recv.at[0, c], across)

    def give_back(c):
        cut = columns(c)
        return remote(res.at[0, :, cut], fin.at[:, cut], pass_send.at[1, c], pass_recv.at[1, c], across)

    def each_column(act):
        def step(c, carry):
            act(c)
            return carry

        lax.fori_loop(0, steps_d, step, 0)

    def block_of(k, c, p):
        return g.at[k, c, p] if k is not None else marks.at[c, p]

    def sem_of(k):
        return k if k is not None else steps_k

    def to_member(k, j):
        block = block_of(k, col, pos)
        return remote(block, block, gather_send.at[sem_of(k), j], gather_recv.at[sem_of(k), j], member(lax.rem(pos + j, line)))

    def from_member(k, j):
        block = block_of(k, col, lax.rem(pos + line - j, line))
        return remote(block, block, gather_send.at[sem_of(k), j], gather_recv.at[sem_of(k), j], partner)

    def to_partner(k, j):
        block = block_of(k, col, lax.rem(pos + line - j, line))
        return remote(block, block, fwd_send.at[sem_of(k), j], fwd_recv.at[sem_of(k), j], partner)

    def from_partner(k, j):
        block = block_of(k, other, lax.rem(pos + line - j, line))
        return remote(block, block, fwd_send.at[sem_of(k), j], fwd_recv.at[sem_of(k), j], partner)

    def send_own(k):
        for j in range(1, line):
            to_member(k, j).start()
        to_partner(k, 0).start()

    def forward(k):
        for j in range(1, line):
            from_member(k, j).wait_recv()
            to_partner(k, j).start()

    def receive(k):
        for j in range(line):
            from_partner(k, j).wait_recv()

    marks[col, pos] = hit[...]
    send_own(None)

    @pl.when(sec == 0)
    def _():
        x[...] = tokens[...]

    @pl.when(sec == 1)
    def _():
        each_column(lambda c: pass_on(c).wait_recv())

    factors = []
    for m in range(2):
        values = x[m].astype(jnp.float32)
        factors.append(lax.rsqrt(jnp.mean(values * values, axis=-1, keepdims=True) + EPSILON))
    for k in range(steps_k):
        for m in range(2):
            values = x[m, :, k * tile_k:(k + 1) * tile_k].astype(jnp.float32)
            normed = values * factors[m] * gain[:, k * tile_k:(k + 1) * tile_k]
            g[k, col, pos, m * half:(m + 1) * half, :] = normed.astype(jnp.bfloat16)
        send_own(k)

    experts = router.shape[1]
    acc[...] = jnp.zeros_like(acc)
    logits[...] = jnp.zeros_like(logits)
    forward(None)
    ahead = min(steps_k, AHEAD)
    for k in range(ahead):
        forward(k)

    def up_step(k, carry):
        @pl.when(k + ahead < steps_k)
        def _():
            forward(k + ahead)

        receive(k)
        lhs = g[k].reshape(total, tile_k)
        at = pl.ds(pl.multiple_of(k * tile_k, tile_k), tile_k)
        logits[...] += lax.dot_general(
            lhs, router[0, :, at], (((1,), (1,)), ((), ())), preferred_element_type=jnp.float32
        )
        for which in range(2):
            load_gu(k, which, False)
            slot = lax.rem(2 * k + which, slots_gu)
            for f in range(steps_f):
                cut = slice(f * tile_f, (f + 1) * tile_f)
                acc[which, :, cut] += jnp.dot(lhs, wgu[slot, :, cut], preferred_element_type=jnp.float32)
            later = 2 * k + which + slots_gu

            @pl.when(later < loads)
            def _():
                if slots_gu % 2 == 0:
                    load_gu(k + slots_gu // 2, which, True)
                elif which == 0:
                    load_gu(k + slots_gu // 2, 1, True)
                else:
                    load_gu(k + slots_gu // 2 + 1, 0, True)

        @pl.when((sec == 0) & (k == start_down))
        def _():
            first_down()

        return carry

    start_down = max(0, (loads - slots_gu - 1) // 2)
    lax.fori_loop(0, steps_k, up_step, 0)

    receive(None)
    routed = marks[...].reshape(total, LANES)[:, 0:experts].astype(jnp.float32)
    picked = jax.nn.sigmoid(logits[...]) * routed
    gates = picked / jnp.sum(picked, axis=-1, keepdims=True)
    lane = lax.broadcasted_iota(jnp.int32, (total, experts), 1)
    for f in range(steps_f):
        cut = slice(f * tile_f, (f + 1) * tile_f)
        expert = lax.div(me * ff_local + f * tile_f, unit_width)
        scale = jnp.sum(jnp.where(lane == expert, gates, 0.0), axis=-1, keepdims=True)
        gate_part = acc[0, :, cut]
        value = gate_part / (1.0 + jnp.exp(-gate_part)) * acc[1, :, cut] * scale
        hidden[:, cut] = value.astype(jnp.bfloat16)

    def pair_copy(c):
        return remote(y.at[c, other], rx.at[c], pair_send.at[c], pair_recv.at[c], partner)

    def line_copy(c, k):
        p = lax.rem(pos + k, line)
        return remote(y.at[c, col, p], rz.at[c, k - 1], line_send.at[c, k - 1], line_recv.at[c, k - 1], member(p))

    def line_step(c):
        pair_copy(c).wait_recv()
        y[c, col] = (y[c, col].astype(jnp.float32) + rx[c].astype(jnp.float32)).astype(jnp.bfloat16)
        for k in range(1, line):
            line_copy(c, k).start()

    def down_step(c, carry):
        load_d(c, False)
        part = jnp.dot(hidden[...], wd[lax.rem(c, slots_d)], preferred_element_type=jnp.float32)
        y[c] = part.astype(jnp.bfloat16).reshape(2, line, rows, tile_d)
        pair_copy(c).start()

        @pl.when(c + slots_d < steps_d)
        def _():
            load_d(c + slots_d, True)

        @pl.when(c >= lag_d)
        def _():
            line_step(c - lag_d)

        return carry

    def late_step(c, carry):
        line_step(c)
        return carry

    lag_d = min(steps_d, LAG)
    lax.fori_loop(0, steps_d, down_step, 0)
    lax.fori_loop(steps_d - lag_d, steps_d, late_step, 0)

    def finish_step(c, carry):
        at = columns(c)
        branch = y[c, col, pos].astype(jnp.float32)
        for k in range(1, line):
            line_copy(c, k).wait_recv()
            branch = branch + rz[c, k - 1].astype(jnp.float32)
        for m in range(2):
            res[m, :, at] = (x[m, :, at].astype(jnp.float32) + branch[m * half:(m + 1) * half]).astype(jnp.bfloat16)

        @pl.when(sec == 0)
        def _():
            pass_on(c).start()

        @pl.when(sec == 1)
        def _():
            give_back(c).start()

        return carry

    lax.fori_loop(0, steps_d, finish_step, 0)

    def drain_own(k):
        for j in range(1, line):
            to_member(k, j).wait_send()
        for j in range(line):
            to_partner(k, j).wait_send()

    def drain_chunk(k, carry):
        drain_own(k)
        return carry

    drain_own(None)
    lax.fori_loop(0, steps_k, drain_chunk, 0)

    def drain_step(c, carry):
        pair_copy(c).wait_send()
        for k in range(1, line):
            line_copy(c, k).wait_send()
        return carry

    lax.fori_loop(0, steps_d, drain_step, 0)

    @pl.when(sec == 0)
    def _():
        each_column(lambda c: pass_on(c).wait_send())
        each_column(lambda c: give_back(c).wait_recv())
        out[0] = fin[...]

    @pl.when(sec == 1)
    def _():
        out[0] = res[1]
        each_column(lambda c: give_back(c).wait_send())


def local(count, tokens, routes, norm_gain, router_weight, gate_weight, up_weight, down_weight):
    micro, per_block, width = tokens.shape
    rows = micro * per_block
    experts = router_weight.shape[-1]
    ff_local = gate_weight.shape[-1]
    unit_width = ff_local * count // experts
    line = count // 2
    tile_k = largest_divisor(width, 1024)
    tile_d = largest_divisor(width, 512)
    steps_k, steps_d = width // tile_k, width // tile_d
    slots_gu, slots_d = min(2 * steps_k, 9), min(steps_d, 6)
    picks = routes[0].reshape(rows, routes.shape[-1])
    hit = jnp.sum(
        (picks[:, :, None] == jnp.arange(LANES, dtype=jnp.int32)).astype(jnp.float32), axis=1
    ).astype(jnp.bfloat16)
    dma = pltpu.SemaphoreType.DMA
    vmem = pl.BlockSpec(memory_space=pltpu.VMEM)
    anyspace = pl.BlockSpec(memory_space=pl.ANY)
    bf16 = jnp.bfloat16
    return pl.pallas_call(
        functools.partial(kernel, count, unit_width, slots_gu, slots_d),
        out_shape=jax.ShapeDtypeStruct((1, per_block, width), bf16),
        in_specs=[vmem, vmem, vmem, vmem, anyspace, anyspace, anyspace],
        out_specs=vmem,
        scratch_shapes=[
            pltpu.VMEM((micro, per_block, width), bf16),
            pltpu.VMEM((steps_k, 2, line, rows, tile_k), bf16),
            pltpu.VMEM((2, line, rows, LANES), bf16),
            pltpu.VMEM((count * rows, experts), jnp.float32),
            pltpu.VMEM((2, count * rows, ff_local), jnp.float32),
            pltpu.VMEM((count * rows, ff_local), bf16),
            pltpu.VMEM((slots_gu, tile_k, ff_local), bf16),
            pltpu.VMEM((slots_d, ff_local, tile_d), bf16),
            pltpu.VMEM((steps_d, 2, line, rows, tile_d), bf16),
            pltpu.VMEM((steps_d, line, rows, tile_d), bf16),
            pltpu.VMEM((steps_d, line - 1, rows, tile_d), bf16),
            pltpu.VMEM((micro, per_block, width), bf16),
            pltpu.VMEM((per_block, width), bf16),
            dma((slots_gu,)),
            dma((slots_d,)),
            dma((steps_k + 1, line)),
            dma((steps_k + 1, line)),
            dma((steps_k + 1, line)),
            dma((steps_k + 1, line)),
            dma((steps_d,)),
            dma((steps_d,)),
            dma((steps_d, line - 1)),
            dma((steps_d, line - 1)),
            dma((2, steps_d)),
            dma((2, steps_d)),
        ],
        compiler_params=pltpu.CompilerParams(
            collective_id=0, has_side_effects=True, vmem_limit_bytes=67043328
        ),
    )(tokens, hit, norm_gain, jnp.swapaxes(router_weight, 1, 2), gate_weight, up_weight, down_weight)


def solution(mesh):
    placed = (
        P(None, ("groups", "expert"), None),
        P("section", None, ("groups", "expert"), None),
        P("section", None),
        P("section", None, None),
        P("section", None, "expert"),
        P("section", None, "expert"),
        P("section", "expert", None),
    )
    return jax.shard_map(
        functools.partial(local, mesh.shape["expert"]),
        mesh=mesh,
        in_specs=placed,
        out_specs=P("section", ("groups", "expert"), None),
        check_vma=False,
    )
```

```python
import functools

import jax
import jax.numpy as jnp
from jax import lax
from jax.experimental import pallas as pl
from jax.experimental.pallas import tpu as pltpu
from jax.sharding import PartitionSpec as P

EPSILON = 1e-06
MESH = pl.DeviceIdType.MESH
LANES = 128
LAG = 5
AHEAD = 3


def largest_divisor(value, most):
    return next(d for d in range(min(value, most), 0, -1) if value % d == 0)


def kernel(
    count, unit_width, slots_gu, slots_d,
    tokens, hit, gain, router, gate_hbm, up_hbm, down_hbm, out,
    x, g, marks, logits, acc, hidden, wgu, wd, y, rx, rz, res, fin,
    sem_gu, sem_d, gather_send, gather_recv, fwd_send, fwd_recv,
    pair_send, pair_recv, line_send, line_recv, pass_send, pass_recv,
):
    me = lax.axis_index("expert")
    sec = lax.axis_index("section")
    line = count // 2
    col, pos = lax.rem(me, 2), lax.div(me, 2)
    other = 1 - col
    width = x.shape[-1]
    tile_k = wgu.shape[1]
    tile_f = largest_divisor(min(unit_width, wgu.shape[-1]), 512)
    steps_k = width // tile_k
    tile_d = wd.shape[-1]
    ff_local = hidden.shape[-1]
    steps_f = ff_local // tile_f
    loads = 2 * steps_k
    steps_d = width // tile_d
    rows = g.shape[3]
    total = count * rows
    half = rows // 2
    partner = {"expert": pos * 2 + other}
    across = {"section": 1 - sec}

    def member(p):
        return {"expert": p * 2 + col}

    def load_gu(k, which, start):
        slot = lax.rem(2 * k + which, slots_gu)
        source = (gate_hbm, up_hbm)[which]
        copy = pltpu.make_async_copy(
            source.at[0, pl.ds(pl.multiple_of(k * tile_k, tile_k), tile_k), :],
            wgu.at[slot],
            sem_gu.at[slot],
        )
        copy.start() if start else copy.wait()

    def load_d(c, start):
        slot = lax.rem(c, slots_d)
        copy = pltpu.make_async_copy(
            down_hbm.at[0, :, pl.ds(pl.multiple_of(c * tile_d, tile_d), tile_d)],
            wd.at[slot],
            sem_d.at[slot],
        )
        copy.start() if start else copy.wait()

    for number in range(slots_gu):
        load_gu(number // 2, number % 2, True)

    def first_down():
        for c in range(slots_d):
            load_d(c, True)

    @pl.when(sec == 1)
    def _():
        first_down()

    barrier = pltpu.get_barrier_semaphore()
    for k in range(1, line):
        pl.semaphore_signal(barrier, inc=1, device_id=member(lax.rem(pos + k, line)), device_id_type=MESH)
    pl.semaphore_signal(barrier, inc=1, device_id=partner, device_id_type=MESH)
    pl.semaphore_signal(barrier, inc=1, device_id=across, device_id_type=MESH)
    pl.semaphore_wait(barrier, line + 1)

    def remote(src, dst, send, recv, device):
        return pltpu.make_async_remote_copy(
            src_ref=src, dst_ref=dst, send_sem=send, recv_sem=recv,
            device_id=device, device_id_type=MESH,
        )

    def columns(c):
        return pl.ds(pl.multiple_of(c * tile_d, tile_d), tile_d)

    def pass_on(c):
        cut = columns(c)
        return remote(res.at[:, :, cut], x.at[:, :, cut], pass_send.at[0, c], pass_recv.at[0, c], across)

    def give_back(c):
        cut = columns(c)
        return remote(res.at[0, :, cut], fin.at[:, cut], pass_send.at[1, c], pass_recv.at[1, c], across)

    def each_column(act):
        def step(c, carry):
            act(c)
            return carry

        lax.fori_loop(0, steps_d, step, 0)

    def block_of(k, c, p):
        return g.at[k, c, p] if k is not None else marks.at[c, p]

    def sem_of(k):
        return k if k is not None else steps_k

    def to_member(k, j):
        block = block_of(k, col, pos)
        return remote(block, block, gather_send.at[sem_of(k), j], gather_recv.at[sem_of(k), j], member(lax.rem(pos + j, line)))

    def from_member(k, j):
        block = block_of(k, col, lax.rem(pos + line - j, line))
        return remote(block, block, gather_send.at[sem_of(k), j], gather_recv.at[sem_of(k), j], partner)

    def to_partner(k, j):
        block = block_of(k, col, lax.rem(pos + line - j, line))
        return remote(block, block, fwd_send.at[sem_of(k), j], fwd_recv.at[sem_of(k), j], partner)

    def from_partner(k, j):
        block = block_of(k, other, lax.rem(pos + line - j, line))
        return remote(block, block, fwd_send.at[sem_of(k), j], fwd_recv.at[sem_of(k), j], partner)

    def send_own(k):
        for j in range(1, line):
            to_member(k, j).start()
        to_partner(k, 0).start()

    def forward(k):
        for j in range(1, line):
            from_member(k, j).wait_recv()
            to_partner(k, j).start()

    def receive(k):
        for j in range(line):
            from_partner(k, j).wait_recv()

    marks[col, pos] = hit[...]
    send_own(None)

    @pl.when(sec == 0)
    def _():
        x[...] = tokens[...]

    @pl.when(sec == 1)
    def _():
        each_column(lambda c: pass_on(c).wait_recv())

    factors = []
    for m in range(2):
        values = x[m].astype(jnp.float32)
        factors.append(lax.rsqrt(jnp.mean(values * values, axis=-1, keepdims=True) + EPSILON))
    for k in range(steps_k):
        for m in range(2):
            values = x[m, :, k * tile_k:(k + 1) * tile_k].astype(jnp.float32)
            normed = values * factors[m] * gain[:, k * tile_k:(k + 1) * tile_k]
            g[k, col, pos, m * half:(m + 1) * half, :] = normed.astype(jnp.bfloat16)
        send_own(k)

    experts = router.shape[1]
    acc[...] = jnp.zeros_like(acc)
    logits[...] = jnp.zeros_like(logits)
    forward(None)
    ahead = min(steps_k, AHEAD)
    for k in range(ahead):
        forward(k)

    def up_step(k, carry):
        @pl.when(k + ahead < steps_k)
        def _():
            forward(k + ahead)

        receive(k)
        lhs = g[k].reshape(total, tile_k)
        at = pl.ds(pl.multiple_of(k * tile_k, tile_k), tile_k)
        logits[...] += lax.dot_general(
            lhs, router[0, :, at], (((1,), (1,)), ((), ())), preferred_element_type=jnp.float32
        )
        for which in range(2):
            load_gu(k, which, False)
            slot = lax.rem(2 * k + which, slots_gu)
            for f in range(steps_f):
                cut = slice(f * tile_f, (f + 1) * tile_f)
                acc[which, :, cut] += jnp.dot(lhs, wgu[slot, :, cut], preferred_element_type=jnp.float32)
            later = 2 * k + which + slots_gu

            @pl.when(later < loads)
            def _():
                if slots_gu % 2 == 0:
                    load_gu(k + slots_gu // 2, which, True)
                elif which == 0:
                    load_gu(k + slots_gu // 2, 1, True)
                else:
                    load_gu(k + slots_gu // 2 + 1, 0, True)

        @pl.when((sec == 0) & (k == start_down))
        def _():
            first_down()

        return carry

    start_down = max(0, (loads - slots_gu - 1) // 2)
    lax.fori_loop(0, steps_k, up_step, 0)

    receive(None)
    routed = marks[...].reshape(total, LANES)[:, 0:experts].astype(jnp.float32)
    picked = jax.nn.sigmoid(logits[...]) * routed
    gates = picked / jnp.sum(picked, axis=-1, keepdims=True)
    lane = lax.broadcasted_iota(jnp.int32, (total, experts), 1)
    for f in range(steps_f):
        cut = slice(f * tile_f, (f + 1) * tile_f)
        expert = lax.div(me * ff_local + f * tile_f, unit_width)
        scale = jnp.sum(jnp.where(lane == expert, gates, 0.0), axis=-1, keepdims=True)
        gate_part = acc[0, :, cut]
        value = gate_part / (1.0 + jnp.exp(-gate_part)) * acc[1, :, cut] * scale
        hidden[:, cut] = value.astype(jnp.bfloat16)

    def pair_copy(c):
        return remote(y.at[c, other], rx.at[c], pair_send.at[c], pair_recv.at[c], partner)

    def line_copy(c, k):
        p = lax.rem(pos + k, line)
        return remote(y.at[c, col, p], rz.at[c, k - 1], line_send.at[c, k - 1], line_recv.at[c, k - 1], member(p))

    def line_step(c):
        pair_copy(c).wait_recv()
        y[c, col] = (y[c, col].astype(jnp.float32) + rx[c].astype(jnp.float32)).astype(jnp.bfloat16)
        for k in range(1, line):
            line_copy(c, k).start()

    def down_step(c, carry):
        load_d(c, False)
        part = jnp.dot(hidden[...], wd[lax.rem(c, slots_d)], preferred_element_type=jnp.float32)
        y[c] = part.astype(jnp.bfloat16).reshape(2, line, rows, tile_d)
        pair_copy(c).start()

        @pl.when(c + slots_d < steps_d)
        def _():
            load_d(c + slots_d, True)

        @pl.when(c >= lag_d)
        def _():
            line_step(c - lag_d)

        return carry

    def late_step(c, carry):
        line_step(c)
        return carry

    lag_d = min(steps_d, LAG)
    lax.fori_loop(0, steps_d, down_step, 0)
    lax.fori_loop(steps_d - lag_d, steps_d, late_step, 0)

    def finish_step(c, carry):
        at = columns(c)
        branch = y[c, col, pos].astype(jnp.float32)
        for k in range(1, line):
            line_copy(c, k).wait_recv()
            branch = branch + rz[c, k - 1].astype(jnp.float32)
        for m in range(2):
            res[m, :, at] = (x[m, :, at].astype(jnp.float32) + branch[m * half:(m + 1) * half]).astype(jnp.bfloat16)

        @pl.when(sec == 0)
        def _():
            pass_on(c).start()

        @pl.when(sec == 1)
        def _():
            give_back(c).start()

        return carry

    lax.fori_loop(0, steps_d, finish_step, 0)

    def drain_own(k):
        for j in range(1, line):
            to_member(k, j).wait_send()
        for j in range(line):
            to_partner(k, j).wait_send()

    def drain_chunk(k, carry):
        drain_own(k)
        return carry

    drain_own(None)
    lax.fori_loop(0, steps_k, drain_chunk, 0)

    def drain_step(c, carry):
        pair_copy(c).wait_send()
        for k in range(1, line):
            line_copy(c, k).wait_send()
        return carry

    lax.fori_loop(0, steps_d, drain_step, 0)

    @pl.when(sec == 0)
    def _():
        each_column(lambda c: pass_on(c).wait_send())
        each_column(lambda c: give_back(c).wait_recv())
        out[0] = fin[...]

    @pl.when(sec == 1)
    def _():
        out[0] = res[1]
        each_column(lambda c: give_back(c).wait_send())


def local(count, tokens, routes, norm_gain, router_weight, gate_weight, up_weight, down_weight):
    micro, per_block, width = tokens.shape
    rows = micro * per_block
    experts = router_weight.shape[-1]
    ff_local = gate_weight.shape[-1]
    unit_width = ff_local * count // experts
    line = count // 2
    tile_k = largest_divisor(width, 1024)
    tile_d = largest_divisor(width, 512)
    steps_k, steps_d = width // tile_k, width // tile_d
    slots_gu, slots_d = min(2 * steps_k, 9), min(steps_d, 6)
    picks = routes[0].reshape(rows, routes.shape[-1])
    hit = jnp.sum(
        (picks[:, :, None] == jnp.arange(LANES, dtype=jnp.int32)).astype(jnp.float32), axis=1
    ).astype(jnp.bfloat16)
    dma = pltpu.SemaphoreType.DMA
    vmem = pl.BlockSpec(memory_space=pltpu.VMEM)
    anyspace = pl.BlockSpec(memory_space=pl.ANY)
    bf16 = jnp.bfloat16
    return pl.pallas_call(
        functools.partial(kernel, count, unit_width, slots_gu, slots_d),
        out_shape=jax.ShapeDtypeStruct((1, per_block, width), bf16),
        in_specs=[vmem, vmem, vmem, vmem, anyspace, anyspace, anyspace],
        out_specs=vmem,
        scratch_shapes=[
            pltpu.VMEM((micro, per_block, width), bf16),
            pltpu.VMEM((steps_k, 2, line, rows, tile_k), bf16),
            pltpu.VMEM((2, line, rows, LANES), bf16),
            pltpu.VMEM((count * rows, experts), jnp.float32),
            pltpu.VMEM((2, count * rows, ff_local), jnp.float32),
            pltpu.VMEM((count * rows, ff_local), bf16),
            pltpu.VMEM((slots_gu, tile_k, ff_local), bf16),
            pltpu.VMEM((slots_d, ff_local, tile_d), bf16),
            pltpu.VMEM((steps_d, 2, line, rows, tile_d), bf16),
            pltpu.VMEM((steps_d, line, rows, tile_d), bf16),
            pltpu.VMEM((steps_d, line - 1, rows, tile_d), bf16),
            pltpu.VMEM((micro, per_block, width), bf16),
            pltpu.VMEM((per_block, width), bf16),
            dma((slots_gu,)),
            dma((slots_d,)),
            dma((steps_k + 1, line)),
            dma((steps_k + 1, line)),
            dma((steps_k + 1, line)),
            dma((steps_k + 1, line)),
            dma((steps_d,)),
            dma((steps_d,)),
            dma((steps_d, line - 1)),
            dma((steps_d, line - 1)),
            dma((2, steps_d)),
            dma((2, steps_d)),
        ],
        compiler_params=pltpu.CompilerParams(
            collective_id=0, has_side_effects=True, vmem_limit_bytes=67043328
        ),
    )(tokens, hit, norm_gain, jnp.swapaxes(router_weight, 1, 2), gate_weight, up_weight, down_weight)


def solution(mesh):
    placed = (
        P(None, ("groups", "expert"), None),
        P("section", None, ("groups", "expert"), None),
        P("section", None),
        P("section", None, None),
        P("section", None, "expert"),
        P("section", None, "expert"),
        P("section", "expert", None),
    )
    return jax.shard_map(
        functools.partial(local, mesh.shape["expert"]),
        mesh=mesh,
        in_specs=placed,
        out_specs=P("section", ("groups", "expert"), None),
        check_vma=False,
    )
```
